1024 devices in a mesh: row: 64 (over y, z_lo, core), col: 16 (over x, z_hi).
Axes of the slice: x: 4, y: 8, z: 16 (z_hi: 4, z_lo: 4; z = z_hi * 4 + z_lo), core: 2. Of those that a mesh axis runs over, the one named last changes fastest.
Arguments:
- left_panels: float32 [3, 512, 65536], P(None, 'col', 'row'), may hold values from -0.0234375 to 0.0234375
- right_panels: float32 [3, 65536, 2048], P(None, 'row', 'col'), may hold values from -6 to 6
- window_tiles: float32 [3, 512, 2048], P(None, 'row', 'col'), may hold values from -6 to 6
Outputs:
- updated: float32 [3, 512, 2048], P(None, 'row', 'col')
The draws below stay inside these ranges and needn't reach their ends.
All inputs are finite; a program needn't handle non-finite values.
Results may differ from the reference program's by a relative error of at most 0.00005.
Values sent between devices are 32-bit elements; how exact they have to be, the bound alone decides.
A program may use at most 32 MiB of HBM per device.

```python
import jax
import jax.numpy as jnp
from jax import lax

ORDER = 65536
ROWS = 512
COLS = 2048


def block_scale(key, extent, shards, smallest, high):
    loudness, own = 1.0, jax.random.fold_in(key, 6)
    for dim, shards_of in shards:
        heights = jnp.exp(jax.random.uniform(jax.random.fold_in(own, dim), (shards_of,), jnp.float32, smallest / len(shards), high / len(shards)))
        loudness = loudness * jnp.repeat(heights, extent[dim] // shards_of).reshape([-1 if axis == dim else 1 for axis in range(len(extent))])
    return loudness


def bell_draw(own_key, shape, scale, bound, cuts=(), dtype=jnp.bfloat16):
    factor_of = block_scale(own_key, shape, cuts, -0.22, 0.18) if cuts else 1.0
    entries = jax.random.normal(own_key, shape, jnp.float32) * scale * factor_of
    return jnp.minimum(jnp.maximum(entries, -bound), bound).astype(dtype)


def setup_inputs(seed: int = 0) -> dict:
    keys = jax.random.split(jax.random.key(seed), 4)
    return {
        "left_panels": bell_draw(keys[0], (3, ROWS, ORDER), ORDER ** -0.5, 0.0234375, ((1, 16), (2, 64)), jnp.float32),
        "right_panels": bell_draw(keys[1], (3, ORDER, COLS), 1.0, 6.0, ((1, 64), (2, 16)), jnp.float32),
        "window_tiles": bell_draw(keys[2], (3, ROWS, COLS), 1.0, 6.0, ((1, 64), (2, 16)), jnp.float32),
    }


def product(left_part, right_part):
    return jnp.dot(left_part, right_part, precision=lax.Precision.HIGHEST, preferred_element_type=jnp.float32)


def reference(left_panels, right_panels, window_tiles):
    square = product(left_panels[0], right_panels[0])
    first = product(left_panels[0], right_panels[1]) + product(left_panels[1], right_panels[0])
    second = product(left_panels[0], right_panels[2]) + product(left_panels[1], right_panels[1]) + product(left_panels[2], right_panels[0])
    return jnp.stack([2.0 * window_tiles[0] - square, 2.0 * window_tiles[1] - first, 2.0 * window_tiles[2] - second])
```

```python
import functools

import jax
import jax.numpy as jnp
from jax import lax
from jax.experimental import pallas as pl
from jax.experimental.pallas import tpu as pltpu
from jax.sharding import PartitionSpec as P

MESH = pl.DeviceIdType.MESH
F32, BF16 = jnp.float32, jnp.bfloat16

NX, NZH, NY, NZL, NC = 4, 4, 8, 4, 2
UNITS, RU = 4, 8
SLOTS = NX * NZH

UP_ORDER = (0, 1, 2, 3)
DOWN_ORDER = (2, 3, 0, 1)


def kernel(
    l_hbm, r_hbm, w_ref, out_ref,
    gath, rv, rb, abuf, part, ybuf, zpart, zbuf,
    l_sem, r_sem, g_send, g_recv, y_send, y_recv, z_send, z_recv,
):
    depth = l_hbm.shape[2]
    cols = r_hbm.shape[2]
    row, col = lax.axis_index("row"), lax.axis_index("col")
    core = lax.rem(row, NC)
    zl = lax.rem(row // NC, NZL)
    y = row // (NC * NZL)
    x, zh = col // NZH, lax.rem(col, NZH)

    def row_of(y_, zl_, core_):
        return (y_ * NZL + zl_) * NC + core_

    def col_of(x_, zh_):
        return x_ * NZH + zh_

    steps = {
        "x+": (row, col_of(lax.rem(x + 1, NX), zh)),
        "x-": (row, col_of(lax.rem(x + NX - 1, NX), zh)),
        "z+": (row, col_of(x, lax.rem(zh + 1, NZH))),
        "z-": (row, col_of(x, lax.rem(zh + NZH - 1, NZH))),
    }
    other = lax.rem(core + 1, NC)

    barrier = pltpu.get_barrier_semaphore()
    peers = list(steps.values())
    for dy in range(NY):
        y_ = lax.rem(y + dy, NY)
        if dy:
            peers.append((row_of(y_, zl, core), col))
        peers.append((row_of(y_, zl, other), col))
    for d in range(1, NZL):
        peers.append((row_of(y, lax.rem(zl + d, NZL), core), col))
    for peer in peers:
        pl.semaphore_signal(barrier, inc=1, device_id=peer, device_id_type=MESH)

    def l_copy(s):
        return pltpu.make_async_copy(l_hbm.at[:, pl.ds(s * RU, RU), :], gath.at[0, s], l_sem.at[s])

    def r_copy(j):
        return pltpu.make_async_copy(r_hbm.at[j], rv.at[j], r_sem.at[j])

    for s in range(UNITS):
        l_copy(s).start()
    for j in range(3):
        r_copy(j).start()
    pl.semaphore_wait(barrier, len(peers))

    sent = []

    def send(step, dx, dz, s):
        if step == "x+":
            to = ((dx - 1) % NX, dz)
        elif step == "x-":
            to = ((dx + 1) % NX, dz)
        elif step == "z+":
            to = (dx, (dz - 1) % NZH)
        else:
            to = (dx, (dz + 1) % NZH)
        dst = to[0] * NZH + to[1]
        if dx == 0 and dz == 0:
            src = l_hbm.at[:, pl.ds(s * RU, RU), :]
        else:
            src = gath.at[dx * NZH + dz, s]
        copy = pltpu.make_async_remote_copy(
            src_ref=src,
            dst_ref=gath.at[dst, s],
            send_sem=g_send.at[len(sent)],
            recv_sem=g_recv.at[dst * UNITS + s],
            device_id=steps[step],
            device_id_type=MESH,
        )
        copy.start()
        sent.append(copy)

    def arrived(dx, dz, s):
        slot = dx * NZH + dz
        pltpu.make_async_remote_copy(
            src_ref=gath.at[slot, s],
            dst_ref=gath.at[slot, s],
            send_sem=g_send.at[0],
            recv_sem=g_recv.at[slot * UNITS + s],
            device_id=steps["x+"],
            device_id_type=MESH,
        ).wait_recv()

    for up, down in zip(UP_ORDER, DOWN_ORDER):
        send("z+", 0, 0, up)
        send("z-", 0, 0, down)
        send("x+", 0, 0, up)
        send("x-", 0, 0, down)

    for j in range(3):
        r_copy(j).wait()
        for k in range(0, depth, 256):
            v = rv[j, k : k + 256]
            hi = v.astype(BF16)
            rb[j, k : k + 256, :cols] = hi
            rb[j, k : k + 256, cols:] = (v - hi.astype(F32)).astype(BF16)

    def compute(slot):
        for p in range(3):
            v = gath[slot, :, p].reshape(UNITS * RU, depth)
            hi = v.astype(BF16)
            abuf[p, 0] = hi
            abuf[p, 1] = (v - hi.astype(F32)).astype(BF16)
        rows = UNITS * RU
        outs = [None] * 3
        for j in range(3):
            n = 3 - j
            prod = jnp.dot(
                abuf[:n].reshape(n * 2 * rows, depth), rb[j], preferred_element_type=F32
            )
            for p in range(n):
                hi = prod[p * 2 * rows : (p * 2 + 1) * rows]
                lo = prod[(p * 2 + 1) * rows : (p * 2 + 2) * rows]
                term = hi[:, :cols] + ((hi[:, cols:] + lo[:, :cols]) + lo[:, cols:])
                outs[p + j] = term if outs[p + j] is None else outs[p + j] + term
        for p in range(3):
            for s in range(UNITS):
                part[slot, s % NC, s // NC, p] = outs[p][s * RU : (s + 1) * RU]

    def place(slot):
        c_ = col_of(lax.rem(x + slot // NZH, NX), lax.rem(zh + slot % NZH, NZH))
        return c_ // 2, lax.rem(c_, 2)

    def y_copy(slot, j):
        y_, half = place(slot)
        core_ = lax.rem(core + j, NC)
        src = lax.rem(y - y_ + NY, NY) * NC + j
        return pltpu.make_async_remote_copy(
            src_ref=part.at[slot, core_],
            dst_ref=ybuf.at[src, half],
            send_sem=y_send.at[slot * NC + j],
            recv_sem=y_recv.at[src * 2 + half],
            device_id=(row_of(y_, zl, core_), col),
            device_id_type=MESH,
        )

    def hand_on(slot):
        y_, half = place(slot)
        y_copy(slot, 1).start()

        @pl.when(y_ != y)
        def _():
            y_copy(slot, 0).start()

        @pl.when(y_ == y)
        def _():
            ybuf[0, half] = part[slot, core]

    def block(dx, dz, units=range(UNITS)):
        for s in units:
            arrived(dx, dz, s)
        slot = dx * NZH + dz
        compute(slot)
        hand_on(slot)

    def relay(dz, units_up, units_down):
        for s in units_up:
            arrived(NX - 1, dz, s)
            send("x+", NX - 1, dz, s)
        for s in units_down:
            arrived(1, dz, s)
            send("x-", 1, dz, s)

    def spread(dz, s):
        arrived(0, dz, s)
        send("x+", 0, dz, s)
        send("x-", 0, dz, s)

    for s in range(UNITS):
        l_copy(s).wait()
    compute(0)
    hand_on(0)

    relay(0, (0,), (2,))
    relay(0, (1,), (3,))
    block(3, 0, (2, 3))
    block(1, 0, (0, 1))
    spread(3, 0), send("z+", 0, 3, 0)
    spread(1, 2), send("z-", 0, 1, 2)
    block(2, 0)
    relay(3, (0,), ())
    relay(1, (), (2,))
    spread(3, 1), send("z+", 0, 3, 1)
    spread(1, 3), send("z-", 0, 1, 3)
    relay(3, (1,), ())
    relay(1, (), (3,))
    spread(3, 2)
    spread(1, 0)
    relay(3, (), (2,))
    relay(1, (0,), ())
    spread(3, 3)
    spread(1, 1)
    relay(3, (), (3,))
    relay(1, (1,), ())
    block(0, 3, ())
    block(0, 1, ())
    block(3, 3, (2, 3))
    block(1, 3, (0, 1))
    block(3, 1, (2, 3))
    block(1, 1, (0, 1))
    spread(2, 0)
    spread(2, 2)
    block(2, 3)
    block(2, 1)
    relay(2, (0,), (2,))
    spread(2, 1)
    spread(2, 3)
    block(0, 2, ())
    relay(2, (1,), (3,))
    block(3, 2, (2, 3))
    block(1, 2, (0, 1))
    block(2, 2)

    for src in range(1, NY * NC):
        for half in range(2):
            pltpu.make_async_remote_copy(
                src_ref=ybuf.at[src, half],
                dst_ref=ybuf.at[src, half],
                send_sem=y_send.at[0],
                recv_sem=y_recv.at[src * 2 + half],
                device_id=steps["x+"],
                device_id_type=MESH,
            ).wait_recv()
    total = ybuf[0]
    for src in range(1, NY * NC):
        total = total + ybuf[src]
    zpart[...] = total.reshape(zpart.shape)

    def z_copy(d):
        zl_ = lax.rem(zl + d, NZL)
        return pltpu.make_async_remote_copy(
            src_ref=zpart.at[zl_],
            dst_ref=zbuf.at[d - 1],
            send_sem=z_send.at[d - 1],
            recv_sem=z_recv.at[d - 1],
            device_id=(row_of(y, zl_, core), col),
            device_id_type=MESH,
        )

    for d in range(1, NZL):
        z_copy(d).start()
    acc = zpart[zl]
    for d in range(1, NZL):
        z_copy(d).wait_recv()
        acc = acc + zbuf[d - 1]
    out_ref[...] = 2.0 * w_ref[...] - acc

    for copy in sent:
        copy.wait_send()
    for slot in range(SLOTS):
        y_, _ = place(slot)
        y_copy(slot, 1).wait_send()

        @pl.when(y_ != y)
        def _():
            y_copy(slot, 0).wait_send()

    for d in range(1, NZL):
        z_copy(d).wait_send()


def on_device(left_panels, right_panels, window_tiles):
    planes, height, depth = left_panels.shape
    cols = right_panels.shape[2]
    dma = pltpu.SemaphoreType.DMA
    return pl.pallas_call(
        kernel,
        out_shape=jax.ShapeDtypeStruct(window_tiles.shape, F32),
        in_specs=[
            pl.BlockSpec(memory_space=pltpu.HBM),
            pl.BlockSpec(memory_space=pltpu.HBM),
            pl.BlockSpec(memory_space=pltpu.VMEM),
        ],
        out_specs=pl.BlockSpec(memory_space=pltpu.VMEM),
        scratch_shapes=[
            pltpu.VMEM((SLOTS, UNITS, planes, RU, depth), F32),
            pltpu.VMEM((planes, depth, cols), F32),
            pltpu.VMEM((planes, depth, 2 * cols), BF16),
            pltpu.VMEM((planes, 2, height, depth), BF16),
            pltpu.VMEM((SLOTS, NC, 2, planes, RU, cols), F32),
            pltpu.VMEM((NY * NC, 2, 2, planes, RU, cols), F32),
            pltpu.VMEM((NZL, planes, RU, cols), F32),
            pltpu.VMEM((NZL - 1, planes, RU, cols), F32),
            dma((UNITS,)),
            dma((3,)),
            dma((60,)),
            dma((SLOTS * UNITS,)),
            dma((SLOTS * NC,)),
            dma((NY * NC * 2,)),
            dma((NZL - 1,)),
            dma((NZL - 1,)),
        ],
        compiler_params=pltpu.CompilerParams(
            collective_id=0, has_side_effects=True, vmem_limit_bytes=40 * 2**20
        ),
    )(left_panels, right_panels, window_tiles)


def solution(mesh):
    return jax.shard_map(
        on_device,
        mesh=mesh,
        in_specs=(P(None, "col", "row"), P(None, "row", "col"), P(None, "row", "col")),
        out_specs=P(None, "row", "col"),
        check_vma=False,
    )
```

```python
import functools

import jax
import jax.numpy as jnp
from jax import lax
from jax.experimental import pallas as pl
from jax.experimental.pallas import tpu as pltpu
from jax.sharding import PartitionSpec as P

MESH = pl.DeviceIdType.MESH
F32, BF16 = jnp.float32, jnp.bfloat16

NX, NZH, NY, NZL, NC = 4, 4, 8, 4, 2
RU = 8
SUB = 4
PIECES = 2
UNITS = SUB * PIECES
SLOTS = NX * NZH
UPS, DOWNS = range(UNITS // 2), range(UNITS // 2, UNITS)
NEAR, FAR = 4, 8

Z_ORDER = (
    (0, 0), (2, 0), (0, 1), (2, 1), (0, 2), (2, 2), (0, 3), (1, 0), (2, 3), (1, 1), (0, 4), (1, 2),
    (0, 5), (1, 3), (0, 6), (1, 4), (0, 7), (1, 5), (3, 0), (1, 6), (3, 1), (1, 7), (3, 2), (3, 3),
)


def z_order(step):
    turn = 0 if step == "z+" else SUB // 2
    return [
        ((g + turn) % SUB * PIECES + i, h) for g, h in Z_ORDER for i in range(PIECES)
    ]


def plan():
    service, lag = 2.0, 1.5 * PIECES
    events, pending = [], []
    done = dict.fromkeys(("x+", "x-", "z+", "z-"), 0.0)
    ready = {(step, u, 0) for step in ("z+", "z-") for u in range(UNITS)}
    to_send = {step: z_order(step) for step in ("z+", "z-")}

    def enter(step, item, at):
        done[step] = max(done[step], at) + service
        pending.append((done[step] + lag, step, item))

    def along_x(step, dx, dz, u, at):
        enter(step, ((dx - 1) % NX if step == "x+" else (dx + 1) % NX, dz, u), at)

    def along_z(step, at):
        while to_send[step] and (step, *to_send[step][0]) in ready:
            enter(step, to_send[step].pop(0), at)

    along_z("z+", 0.0)
    along_z("z-", 0.0)
    for up, down in zip([*UPS, *DOWNS], [*DOWNS, *UPS]):
        along_x("x+", 0, 0, up, 0.0)
        along_x("x-", 0, 0, down, 0.0)
    while pending:
        pending.sort()
        at, step, item = pending.pop(0)
        events.append((step, *item))
        if step in to_send:
            u, h = item
            ready.add((step, u, h + 1))
            along_z(step, at)
            if h + 1 in (NEAR, FAR):
                dz = 2 if h + 1 == FAR else NZH - 1 if step == "z+" else 1
                along_x("x+", 0, dz, u, at)
                along_x("x-", 0, dz, u, at)
        else:
            dx, dz, u = item
            if step == "x+" and dx == NX - 1 and u in UPS or step == "x-" and dx == 1 and u in DOWNS:
                along_x(step, dx, dz, u, at)
    return events


def kernel(
    l_hbm, r_hbm, w_ref, out_ref,
    gath, passing, rv, rb, abuf, part, ybuf, zpart, zbuf,
    l_sem, r_sem, g_send, g_recv, p_recv, y_send, y_recv, z_send, z_recv,
):
    depth = l_hbm.shape[2]
    cols = r_hbm.shape[2]
    row, col = lax.axis_index("row"), lax.axis_index("col")
    core = lax.rem(row, NC)
    zl = lax.rem(row // NC, NZL)
    y = row // (NC * NZL)
    x, zh = col // NZH, lax.rem(col, NZH)

    def row_of(y_, zl_, core_):
        return (y_ * NZL + zl_) * NC + core_

    def col_of(x_, zh_):
        return x_ * NZH + zh_

    steps = {
        "x+": (row, col_of(lax.rem(x + 1, NX), zh)),
        "x-": (row, col_of(lax.rem(x + NX - 1, NX), zh)),
    }
    for step, move in (("z+", 1), ("z-", NZH * NZL - 1)):
        z_ = lax.rem(zh * NZL + zl + move, NZH * NZL)
        steps[step] = (row_of(y, lax.rem(z_, NZL), core), col_of(x, z_ // NZL))
    other = lax.rem(core + 1, NC)

    barrier = pltpu.get_barrier_semaphore()
    peers = list(steps.values())
    for dy in range(NY):
        y_ = lax.rem(y + dy, NY)
        if dy:
            peers.append((row_of(y_, zl, core), col))
        peers.append((row_of(y_, zl, other), col))
    for d in range(1, NZL):
        peers.append((row_of(y, lax.rem(zl + d, NZL), core), col))
    for peer in peers:
        pl.semaphore_signal(barrier, inc=1, device_id=peer, device_id_type=MESH)

    def l_copy(s):
        return pltpu.make_async_copy(l_hbm.at[:, pl.ds(s * RU, RU), :], gath.at[0, s], l_sem.at[s])

    def r_copy(j):
        return pltpu.make_async_copy(r_hbm.at[j], rv.at[j], r_sem.at[j])

    for s in range(SUB):
        l_copy(s).start()
    for j in range(3):
        r_copy(j).start()
    pl.semaphore_wait(barrier, len(peers))

    sent = []
    piece = depth // PIECES

    def unit(slot, s):
        return gath.at[slot, s // PIECES, :, :, pl.ds(s % PIECES * piece, piece)]

    def own(s):
        return l_hbm.at[:, pl.ds(s // PIECES * RU, RU), pl.ds(s % PIECES * piece, piece)]

    def start(src, dst, recv_sem, step):
        copy = pltpu.make_async_remote_copy(
            src_ref=src,
            dst_ref=dst,
            send_sem=g_send.at[len(sent)],
            recv_sem=recv_sem,
            device_id=steps[step],
            device_id_type=MESH,
        )
        copy.start()
        sent.append(copy)

    def wait(ref, recv_sem):
        pltpu.make_async_remote_copy(
            src_ref=ref,
            dst_ref=ref,
            send_sem=g_send.at[0],
            recv_sem=recv_sem,
            device_id=steps["x+"],
            device_id_type=MESH,
        ).wait_recv()

    def held(slot, s):
        return unit(slot, s), g_recv.at[slot * UNITS + s]

    def reached(step, s, h):
        if h == NEAR:
            return held(NZH - 1 if step == "z+" else 1, s)
        if h == FAR:
            return held(2, s)
        place_ = ((0 if step == "z+" else 1) * FAR + h) * UNITS + s
        return passing.at[place_ // PIECES, :, :, pl.ds(s % PIECES * piece, piece)], p_recv.at[place_]

    to_send = {step: z_order(step) for step in ("z+", "z-")}
    ready = {(step, u, 0) for step in to_send for u in range(UNITS)}

    def send_z(step):
        while to_send[step] and (step, *to_send[step][0]) in ready:
            u, h = to_send[step].pop(0)
            start(reached(step, u, h)[0] if h else own(u), *reached(step, u, h + 1), step)

    def send_x(step, dx, dz, s):
        to = (dx - 1) % NX if step == "x+" else (dx + 1) % NX
        start(unit(dx * NZH + dz, s) if dx or dz else own(s), *held(to * NZH + dz, s), step)

    send_z("z+")
    send_z("z-")
    for up, down in zip([*UPS, *DOWNS], [*DOWNS, *UPS]):
        send_x("x+", 0, 0, up)
        send_x("x-", 0, 0, down)

    for j in range(3):
        r_copy(j).wait()
        for k in range(0, depth, 256):
            v = rv[j, k : k + 256]
            hi = v.astype(BF16)
            rb[j, k : k + 256, :cols] = hi
            rb[j, k : k + 256, cols:] = (v - hi.astype(F32)).astype(BF16)

    def compute(slot):
        for p in range(3):
            v = gath[slot, :, p].reshape(SUB * RU, depth)
            hi = v.astype(BF16)
            abuf[p, 0] = hi
            abuf[p, 1] = (v - hi.astype(F32)).astype(BF16)
        rows = SUB * RU
        outs = [None] * 3
        for j in range(3):
            n = 3 - j
            prod = jnp.dot(
                abuf[:n].reshape(n * 2 * rows, depth), rb[j], preferred_element_type=F32
            )
            for p in range(n):
                hi = prod[p * 2 * rows : (p * 2 + 1) * rows]
                lo = prod[(p * 2 + 1) * rows : (p * 2 + 2) * rows]
                term = hi[:, :cols] + ((hi[:, cols:] + lo[:, :cols]) + lo[:, cols:])
                outs[p + j] = term if outs[p + j] is None else outs[p + j] + term
        for p in range(3):
            for s in range(SUB):
                part[slot, s % NC, s // NC, p] = outs[p][s * RU : (s + 1) * RU]

    def place(slot):
        c_ = col_of(lax.rem(x + slot // NZH, NX), lax.rem(zh + slot % NZH, NZH))
        return c_ // 2, lax.rem(c_, 2)

    def y_copy(slot, j):
        y_, half = place(slot)
        core_ = lax.rem(core + j, NC)
        src = lax.rem(y - y_ + NY, NY) * NC + j
        return pltpu.make_async_remote_copy(
            src_ref=part.at[slot, core_],
            dst_ref=ybuf.at[src, half],
            send_sem=y_send.at[slot * NC + j],
            recv_sem=y_recv.at[src * 2 + half],
            device_id=(row_of(y_, zl, core_), col),
            device_id_type=MESH,
        )

    def hand_on(slot):
        y_, half = place(slot)
        y_copy(slot, 1).start()

        @pl.when(y_ != y)
        def _():
            y_copy(slot, 0).start()

        @pl.when(y_ == y)
        def _():
            ybuf[0, half] = part[slot, core]

    for s in range(SUB):
        l_copy(s).wait()
    compute(0)
    hand_on(0)

    left = {}
    for step, *item in plan():
        if step in to_send:
            u, h = item
            wait(*reached(step, u, h + 1))
            ready.add((step, u, h + 1))
            send_z(step)
            if h + 1 not in (NEAR, FAR):
                continue
            dx, dz = 0, 2 if h + 1 == FAR else NZH - 1 if step == "z+" else 1
            send_x("x+", dx, dz, u)
            send_x("x-", dx, dz, u)
        else:
            dx, dz, u = item
            wait(*held(dx * NZH + dz, u))
            if step == "x+" and dx == NX - 1 and u in UPS or step == "x-" and dx == 1 and u in DOWNS:
                send_x(step, dx, dz, u)
        left[dx, dz] = left.get((dx, dz), UNITS) - 1
        if not left[dx, dz]:
            compute(dx * NZH + dz)
            hand_on(dx * NZH + dz)

    for src in range(1, NY * NC):
        for half in range(2):
            pltpu.make_async_remote_copy(
                src_ref=ybuf.at[src, half],
                dst_ref=ybuf.at[src, half],
                send_sem=y_send.at[0],
                recv_sem=y_recv.at[src * 2 + half],
                device_id=steps["x+"],
                device_id_type=MESH,
            ).wait_recv()
    total = ybuf[0]
    for src in range(1, NY * NC):
        total = total + ybuf[src]
    zpart[...] = total.reshape(zpart.shape)

    def z_copy(d):
        zl_ = lax.rem(zl + d, NZL)
        return pltpu.make_async_remote_copy(
            src_ref=zpart.at[zl_],
            dst_ref=zbuf.at[d - 1],
            send_sem=z_send.at[d - 1],
            recv_sem=z_recv.at[d - 1],
            device_id=(row_of(y, zl_, core), col),
            device_id_type=MESH,
        )

    for d in range(1, NZL):
        z_copy(d).start()
    acc = zpart[zl]
    for d in range(1, NZL):
        z_copy(d).wait_recv()
        acc = acc + zbuf[d - 1]
    out_ref[...] = 2.0 * w_ref[...] - acc

    for copy in sent:
        copy.wait_send()
    for slot in range(SLOTS):
        y_, _ = place(slot)
        y_copy(slot, 1).wait_send()

        @pl.when(y_ != y)
        def _():
            y_copy(slot, 0).wait_send()

    for d in range(1, NZL):
        z_copy(d).wait_send()


def on_device(left_panels, right_panels, window_tiles):
    planes, height, depth = left_panels.shape
    cols = right_panels.shape[2]
    dma = pltpu.SemaphoreType.DMA
    return pl.pallas_call(
        kernel,
        out_shape=jax.ShapeDtypeStruct(window_tiles.shape, F32),
        in_specs=[
            pl.BlockSpec(memory_space=pltpu.HBM),
            pl.BlockSpec(memory_space=pltpu.HBM),
            pl.BlockSpec(memory_space=pltpu.VMEM),
        ],
        out_specs=pl.BlockSpec(memory_space=pltpu.VMEM),
        scratch_shapes=[
            pltpu.VMEM((SLOTS, SUB, planes, RU, depth), F32),
            pltpu.VMEM((2 * FAR * SUB, planes, RU, depth), F32),
            pltpu.VMEM((planes, depth, cols), F32),
            pltpu.VMEM((planes, depth, 2 * cols), BF16),
            pltpu.VMEM((planes, 2, height, depth), BF16),
            pltpu.VMEM((SLOTS, NC, 2, planes, RU, cols), F32),
            pltpu.VMEM((NY * NC, 2, 2, planes, RU, cols), F32),
            pltpu.VMEM((NZL, planes, RU, cols), F32),
            pltpu.VMEM((NZL - 1, planes, RU, cols), F32),
            dma((SUB,)),
            dma((3,)),
            dma((24 * UNITS,)),
            dma((SLOTS * UNITS,)),
            dma((2 * FAR * UNITS,)),
            dma((SLOTS * NC,)),
            dma((NY * NC * 2,)),
            dma((NZL - 1,)),
            dma((NZL - 1,)),
        ],
        compiler_params=pltpu.CompilerParams(
            collective_id=0, has_side_effects=True, vmem_limit_bytes=62 * 2**20
        ),
    )(left_panels, right_panels, window_tiles)


def solution(mesh):
    return jax.shard_map(
        on_device,
        mesh=mesh,
        in_specs=(P(None, "col", "row"), P(None, "row", "col"), P(None, "row", "col")),
        out_specs=P(None, "row", "col"),
        check_vma=False,
    )
```

```python
import functools

import jax
import jax.numpy as jnp
from jax import lax
from jax.experimental import pallas as pl
from jax.experimental.pallas import tpu as pltpu
from jax.sharding import PartitionSpec as P

MESH = pl.DeviceIdType.MESH
F32, BF16 = jnp.float32, jnp.bfloat16

NX, NZH, NY, NZL, NC = 4, 4, 8, 4, 2
RU = 8
SUB = 4
PIECES = 2
UNITS = SUB * PIECES
SLOTS = NX * NZH
UPS, DOWNS = range(UNITS // 2), range(UNITS // 2, UNITS)
NEAR, FAR = 4, 8

Z_ORDER = (
    (0, 0), (2, 0), (1, 0), (0, 1), (1, 1), (0, 2), (1, 2), (2, 1), (0, 3), (2, 2), (0, 4), (1, 3),
    (0, 5), (2, 3), (1, 4), (0, 6), (1, 5), (0, 7), (1, 6), (3, 0), (1, 7), (3, 1), (3, 2), (3, 3),
)


def z_order(step):
    turn = 0 if step == "z+" else SUB // 2
    return [
        ((g + turn) % SUB * PIECES + i, h) for g, h in Z_ORDER for i in range(PIECES)
    ]


def plan():
    service, lag = 2.0, 2.0 * PIECES
    events, pending = [], []
    done = dict.fromkeys(("x+", "x-", "z+", "z-"), 0.0)
    ready = {(step, u, 0) for step in ("z+", "z-") for u in range(UNITS)}
    to_send = {step: z_order(step) for step in ("z+", "z-")}

    def enter(step, item, at):
        done[step] = max(done[step], at) + service
        pending.append((done[step] + lag, step, item))

    def along_x(step, dx, dz, u, at):
        enter(step, ((dx - 1) % NX if step == "x+" else (dx + 1) % NX, dz, u), at)

    def along_z(step, at):
        while to_send[step] and (step, *to_send[step][0]) in ready:
            enter(step, to_send[step].pop(0), at)

    along_z("z+", 0.0)
    along_z("z-", 0.0)
    for up, down in zip([*UPS, *DOWNS], [*DOWNS, *UPS]):
        along_x("x+", 0, 0, up, 0.0)
        along_x("x-", 0, 0, down, 0.0)
    while pending:
        pending.sort()
        at, step, item = pending.pop(0)
        events.append((step, *item))
        if step in to_send:
            u, h = item
            ready.add((step, u, h + 1))
            along_z(step, at)
            if h + 1 in (NEAR, FAR):
                dz = 2 if h + 1 == FAR else NZH - 1 if step == "z+" else 1
                along_x("x+", 0, dz, u, at)
                along_x("x-", 0, dz, u, at)
        else:
            dx, dz, u = item
            if step == "x+" and dx == NX - 1 and u in UPS or step == "x-" and dx == 1 and u in DOWNS:
                along_x(step, dx, dz, u, at)
    return events


def kernel(
    l_hbm, r_hbm, w_ref, out_ref,
    gath, passing, rv, rb, abuf, part, ybuf, zpart, zbuf,
    l_sem, r_sem, g_send, g_recv, p_recv, y_send, y_recv, z_send, z_recv, word,
):
    depth = l_hbm.shape[2]
    cols = r_hbm.shape[2]
    row, col = lax.axis_index("row"), lax.axis_index("col")
    core = lax.rem(row, NC)
    zl = lax.rem(row // NC, NZL)
    y = row // (NC * NZL)
    x, zh = col // NZH, lax.rem(col, NZH)

    def row_of(y_, zl_, core_):
        return (y_ * NZL + zl_) * NC + core_

    def col_of(x_, zh_):
        return x_ * NZH + zh_

    steps = {
        "x+": (row, col_of(lax.rem(x + 1, NX), zh)),
        "x-": (row, col_of(lax.rem(x + NX - 1, NX), zh)),
    }
    for step, move in (("z+", 1), ("z-", NZH * NZL - 1)):
        z_ = lax.rem(zh * NZL + zl + move, NZH * NZL)
        steps[step] = (row_of(y, lax.rem(z_, NZL), core), col_of(x, z_ // NZL))
    other = lax.rem(core + 1, NC)

    barrier = pltpu.get_barrier_semaphore()
    for step, move in (("y+", 1), ("y-", NY - 1)):
        steps[step] = (row_of(lax.rem(y + move, NY), zl, core), col)
    peers = [*steps.values(), (row_of(y, zl, other), col)]
    for peer in peers:
        pl.semaphore_signal(barrier, inc=1, device_id=peer, device_id_type=MESH)

    rounds = {"y+": NY // 2, "y-": NY // 2, "z+": NZL - 1, "z-": NZL - 1}

    def tell(r):
        for i, step in enumerate(rounds):
            if r < rounds[step]:
                pl.semaphore_signal(word.at[i], inc=1, device_id=steps[step], device_id_type=MESH)

    def hear(r):
        for i, step in enumerate(rounds):
            if r < rounds[step]:
                pl.semaphore_wait(word.at[i], 1)

    piece = depth // PIECES

    def own(s):
        return l_hbm.at[:, pl.ds(s // PIECES * RU, RU), pl.ds(s % PIECES * piece, piece)]

    def l_copy(s):
        return pltpu.make_async_copy(own(s), gath.at[0, s // PIECES, s % PIECES], l_sem.at[s])

    def r_copy(j):
        return pltpu.make_async_copy(r_hbm.at[j], rv.at[j], r_sem.at[j])

    for s in range(UNITS):
        l_copy(s).start()
    for j in range(3):
        r_copy(j).start()
    pl.semaphore_wait(barrier, len(peers))
    tell(0)

    sent = []

    def unit(slot, s):
        return gath.at[slot, s // PIECES, s % PIECES]

    def start(src, dst, recv_sem, step):
        copy = pltpu.make_async_remote_copy(
            src_ref=src,
            dst_ref=dst,
            send_sem=g_send.at[len(sent)],
            recv_sem=recv_sem,
            device_id=steps[step],
            device_id_type=MESH,
        )
        copy.start()
        sent.append(copy)

    def wait(ref, recv_sem):
        pltpu.make_async_remote_copy(
            src_ref=ref,
            dst_ref=ref,
            send_sem=g_send.at[0],
            recv_sem=recv_sem,
            device_id=steps["x+"],
            device_id_type=MESH,
        ).wait_recv()

    def held(slot, s):
        return unit(slot, s), g_recv.at[slot * UNITS + s]

    def reached(step, s, h):
        if h == NEAR:
            return held(NZH - 1 if step == "z+" else 1, s)
        if h == FAR:
            return held(2, s)
        place_ = ((0 if step == "z+" else 1) * FAR + h) * UNITS + s
        return passing.at[place_], p_recv.at[place_]

    to_send = {step: z_order(step) for step in ("z+", "z-")}
    ready = {(step, u, 0) for step in to_send for u in range(UNITS)}

    def send_z(step):
        while to_send[step] and (step, *to_send[step][0]) in ready:
            u, h = to_send[step].pop(0)
            start(reached(step, u, h)[0] if h else own(u), *reached(step, u, h + 1), step)

    def send_x(step, dx, dz, s):
        to = (dx - 1) % NX if step == "x+" else (dx + 1) % NX
        start(unit(dx * NZH + dz, s) if dx or dz else own(s), *held(to * NZH + dz, s), step)

    send_z("z+")
    send_z("z-")
    for up, down in zip([*UPS, *DOWNS], [*DOWNS, *UPS]):
        send_x("x+", 0, 0, up)
        send_x("x-", 0, 0, down)

    for j in range(3):
        r_copy(j).wait()
        for k in range(0, depth, 256):
            v = rv[j, k : k + 256]
            hi = v.astype(BF16)
            rb[j, k : k + 256, :cols] = hi
            rb[j, k : k + 256, cols:] = (v - hi.astype(F32)).astype(BF16)

    def compute(slot, h):
        for p in range(3):
            for i in range(PIECES):
                v = gath[slot, h * NC : (h + 1) * NC, i, p].reshape(NC * RU, piece)
                hi = v.astype(BF16)
                ks = slice(i * piece, (i + 1) * piece)
                abuf[p, 0, :, ks] = hi
                abuf[p, 1, :, ks] = (v - hi.astype(F32)).astype(BF16)
        rows = NC * RU
        outs = [None] * 3
        for j in range(3):
            n = 3 - j
            prod = jnp.dot(
                abuf[:n].reshape(n * 2 * rows, depth), rb[j], preferred_element_type=F32
            )
            for p in range(n):
                hi = prod[p * 2 * rows : (p * 2 + 1) * rows]
                lo = prod[(p * 2 + 1) * rows : (p * 2 + 2) * rows]
                term = hi[:, :cols] + ((hi[:, cols:] + lo[:, :cols]) + lo[:, cols:])
                outs[p + j] = term if outs[p + j] is None else outs[p + j] + term
        for p in range(3):
            for s in range(NC):
                part[slot, s, h, p] = outs[p][s * RU : (s + 1) * RU]

    def place(slot):
        c_ = col_of(lax.rem(x + slot // NZH, NX), lax.rem(zh + slot % NZH, NZH))
        return c_ // 2, lax.rem(c_, 2)

    def y_copy(slot, j, h):
        y_, half = place(slot)
        core_ = lax.rem(core + j, NC)
        src = lax.rem(y - y_ + NY, NY) * NC + j
        return pltpu.make_async_remote_copy(
            src_ref=part.at[slot, core_, h],
            dst_ref=ybuf.at[src, half, h],
            send_sem=y_send.at[(slot * NC + j) * 2 + h],
            recv_sem=y_recv.at[(src * 2 + half) * 2 + h],
            device_id=(row_of(y_, zl, core_), col),
            device_id_type=MESH,
        )

    def hand_on(slot, h):
        y_, half = place(slot)
        y_copy(slot, 1, h).start()

        @pl.when(y_ != y)
        def _():
            y_copy(slot, 0, h).start()

        @pl.when(y_ == y)
        def _():
            ybuf[0, half, h] = part[slot, core, h]

    for s in range(UNITS):
        l_copy(s).wait()
    ended = [(0, 0), (0, 1)]
    for slot, h in ended:
        compute(slot, h)

    left = {}
    for count, (step, *item) in enumerate(plan()):
        if count % 6 == 5 and count // 6 < NY // 2:
            hear(count // 6)
            tell(count // 6 + 1)
        if step in to_send:
            u, h = item
            wait(*reached(step, u, h + 1))
            ready.add((step, u, h + 1))
            send_z(step)
            if h + 1 not in (NEAR, FAR):
                continue
            dx, dz = 0, 2 if h + 1 == FAR else NZH - 1 if step == "z+" else 1
            send_x("x+", dx, dz, u)
            send_x("x-", dx, dz, u)
        else:
            dx, dz, u = item
            wait(*held(dx * NZH + dz, u))
            if step == "x+" and dx == NX - 1 and u in UPS or step == "x-" and dx == 1 and u in DOWNS:
                send_x(step, dx, dz, u)
        h = u // (UNITS // 2)
        left[dx, dz, h] = left.get((dx, dz, h), UNITS // 2) - 1
        if not left[dx, dz, h]:
            compute(dx * NZH + dz, h)
            ended.append((dx * NZH + dz, h))
        if count >= 6 * (NY // 2):
            while ended:
                hand_on(*ended.pop(0))

    for src in range(1, NY * NC):
        for i in range(4):
            wait(ybuf.at[src, i // 2, i % 2], y_recv.at[src * 4 + i])
    total = ybuf[0]
    for src in range(1, NY * NC):
        total = total + ybuf[src]
    zpart[...] = total.reshape(zpart.shape)

    def z_copy(d):
        zl_ = lax.rem(zl + d, NZL)
        return pltpu.make_async_remote_copy(
            src_ref=zpart.at[zl_],
            dst_ref=zbuf.at[d - 1],
            send_sem=z_send.at[d - 1],
            recv_sem=z_recv.at[d - 1],
            device_id=(row_of(y, zl_, core), col),
            device_id_type=MESH,
        )

    for d in range(1, NZL):
        z_copy(d).start()
    acc = zpart[zl]
    for d in range(1, NZL):
        z_copy(d).wait_recv()
        acc = acc + zbuf[d - 1]
    out_ref[...] = 2.0 * w_ref[...] - acc

    for copy in sent:
        copy.wait_send()
    for slot in range(SLOTS):
        y_, _ = place(slot)
        for h in range(2):
            y_copy(slot, 1, h).wait_send()

        @pl.when(y_ != y)
        def _():
            for h in range(2):
                y_copy(slot, 0, h).wait_send()

    for d in range(1, NZL):
        z_copy(d).wait_send()


def on_device(left_panels, right_panels, window_tiles):
    planes, height, depth = left_panels.shape
    cols = right_panels.shape[2]
    dma = pltpu.SemaphoreType.DMA
    return pl.pallas_call(
        kernel,
        out_shape=jax.ShapeDtypeStruct(window_tiles.shape, F32),
        in_specs=[
            pl.BlockSpec(memory_space=pltpu.HBM),
            pl.BlockSpec(memory_space=pltpu.HBM),
            pl.BlockSpec(memory_space=pltpu.VMEM),
        ],
        out_specs=pl.BlockSpec(memory_space=pltpu.VMEM),
        scratch_shapes=[
            pltpu.VMEM((SLOTS, SUB, PIECES, planes, RU, depth // PIECES), F32),
            pltpu.VMEM((2 * FAR * UNITS, planes, RU, depth // PIECES), F32),
            pltpu.VMEM((planes, depth, cols), F32),
            pltpu.VMEM((planes, depth, 2 * cols), BF16),
            pltpu.VMEM((planes, 2, NC * RU, depth), BF16),
            pltpu.VMEM((SLOTS, NC, 2, planes, RU, cols), F32),
            pltpu.VMEM((NY * NC, 2, 2, planes, RU, cols), F32),
            pltpu.VMEM((NZL, planes, RU, cols), F32),
            pltpu.VMEM((NZL - 1, planes, RU, cols), F32),
            dma((UNITS,)),
            dma((3,)),
            dma((24 * UNITS,)),
            dma((SLOTS * UNITS,)),
            dma((2 * FAR * UNITS,)),
            dma((SLOTS * NC * 2,)),
            dma((NY * NC * 4,)),
            dma((NZL - 1,)),
            dma((NZL - 1,)),
            pltpu.SemaphoreType.REGULAR((4,)),
        ],
        compiler_params=pltpu.CompilerParams(
            collective_id=0, has_side_effects=True, vmem_limit_bytes=62 * 2**20
        ),
    )(left_panels, right_panels, window_tiles)


def solution(mesh):
    return jax.shard_map(
        on_device,
        mesh=mesh,
        in_specs=(P(None, "col", "row"), P(None, "row", "col"), P(None, "row", "col")),
        out_specs=P(None, "row", "col"),
        check_vma=False,
    )
```
